32 devices in a mesh: ctx: 8 (over z, x), head: 4 (over y, core).
Axes of the slice: x: 2, y: 2, z: 4, core: 2. Of those that a mesh axis runs over, the one named last changes fastest.
Arguments:
- queries: bfloat16 [256, 128, 128], P('head'), may hold values from -48 to 48
- keys: bfloat16 [8, 65536, 128], P('head', 'ctx'), may hold values from -6 to 6
- values: bfloat16 [8, 65536, 128], P('head', 'ctx'), may hold values from -6 to 6
- key_block_scale: float32 [8, 1024], P('head', 'ctx'), may hold values from 0.5 to 2
- value_block_scale: float32 [8, 1024], P('head', 'ctx'), may hold values from 0.5 to 2
- selection: int32 [8, 128], P('head'), may hold values from 0 to 1023, as said below
Outputs:
- attended: bfloat16 [256, 128, 128], P('ctx', 'head')
The draws below stay inside these ranges and needn't reach their ends.
Inputs may be any that keep to these rules, and one draw needn't show every extreme that they name: `selection`: each row lists 128 distinct block numbers in increasing order. Of the blocks i * 128 to (i + 1) * 128 - 1, a row lists between 1 and 40, and exactly 40 for some i in every row.
All inputs are finite; a program needn't handle non-finite values.
Results may differ from the reference program's by a relative error of at most 0.017.
Values may be sent and summed in bfloat16 or wider, within the bound.
No kernel may reach another device: no remote copies, remote signals or barrier semaphores. Data moves between devices by JAX's collectives and lax.ppermute only.
A program may use at most 192 MiB of HBM per device.

```python
import math
import jax
import jax.numpy as jnp
from jax import lax

HQ = 128
KEY_VALUE_HEADS = 8
HEAD_SIZE = 128
BLK = 64
QUERY_TOKENS = 256
QUERY_PER_KEY = 16
NBLK_DEV = 128
SEL_DEV = 16
MOST = 40
CONTEXT_TOKENS = 65536
CONTEXT_BLOCKS = 1024
SEL = 128


def draw_queries(key, part):
    inner = jax.random.fold_in(key, 101)
    base = jax.random.normal(inner, (QUERY_TOKENS, HQ, HEAD_SIZE), jnp.float32)
    drawn = jnp.clip(base, -48.0, 48.0)
    return drawn.astype(jnp.bfloat16)


def one_row(row_key):
    shards = CONTEXT_BLOCKS // NBLK_DEV
    first, second, third = jax.random.split(row_key, 3)
    order = jax.random.permutation(first, shards)
    rank = jnp.zeros((shards,), jnp.int32).at[order].set(jnp.arange(shards, dtype=jnp.int32))
    excess = MOST - SEL_DEV
    sizes = jax.random.randint(second, (shards,), 0, SEL_DEV // 2 + 1)
    paired = jnp.clip((rank - 3) // 2, 0, shards - 1)
    signed = jnp.where((rank - 3) % 2 == 0, 1, -1) * sizes[paired]
    alone = (rank == shards - 1) & ((shards - 3) % 2 == 1)
    delta = jnp.where(rank == 0, excess, jnp.where(rank == 1, -(excess // 2), jnp.where(rank == 2, -(excess - excess // 2), jnp.where(alone, 0, signed))))
    counts = SEL_DEV + delta
    perms = jax.vmap(lambda shard_key: jax.random.permutation(shard_key, NBLK_DEV))(jax.random.split(third, shards))
    chosen = (perms < counts[:, None]).reshape(-1)
    places = jnp.arange(CONTEXT_BLOCKS, dtype=jnp.int32)
    ordered = jnp.sort(jnp.where(chosen, places, CONTEXT_BLOCKS + places))
    return ordered[:SEL].astype(jnp.int32)


def draw_selection(key, part):
    keys_per_row = jax.random.split(jax.random.fold_in(key, 202), KEY_VALUE_HEADS)
    return jax.vmap(one_row)(keys_per_row)


def block_levels(own_key, dims, cuts, least, high):
    def one(axis_at, shards_of):
        steps = jax.random.uniform(jax.random.fold_in(jax.random.fold_in(own_key, 6), axis_at), (shards_of,), jnp.float32, least / len(cuts), high / len(cuts))
        return jnp.repeat(jnp.exp(steps), dims[axis_at] // shards_of).reshape((-1,) + (1,) * (len(dims) - axis_at - 1))

    loudness = one(*cuts[0])
    for cut in cuts[1:]:
        loudness = loudness * one(*cut)
    return loudness


def scatter_about(key, dims, deviation, limit, cuts=(), held_as=jnp.bfloat16):
    values = jax.random.normal(key, dims, jnp.float32) * deviation
    if len(cuts) > 0:
        values = block_levels(key, dims, cuts, -0.22, 0.18) * values
    return jnp.clip(values, min=-limit, max=limit).astype(held_as)


def setup_inputs(seed: int = 0) -> dict:
    key_of = jax.random.split(jax.random.key(seed), 7)
    queries = draw_queries(jax.random.fold_in(key_of[6], 71), 0)
    keys = scatter_about(key_of[1], (KEY_VALUE_HEADS, CONTEXT_TOKENS, HEAD_SIZE), 1.0, 6.0, ((0, 4), (1, 8)))
    values = scatter_about(key_of[2], (KEY_VALUE_HEADS, CONTEXT_TOKENS, HEAD_SIZE), 1.0, 6.0, ((0, 4), (1, 8)))
    key_block_scale = jnp.clip(jnp.exp(math.log(2.0) - 1.3862944 * jax.random.uniform(key_of[3], (KEY_VALUE_HEADS, CONTEXT_BLOCKS), jnp.float32) ** block_levels(key_of[3], (KEY_VALUE_HEADS, CONTEXT_BLOCKS), ((0, 4), (1, 8)), -0.2, 0.2)), 0.5, 2.0)
    value_block_scale = jnp.clip(jnp.exp(math.log(2.0) - 1.3862944 * jax.random.uniform(key_of[4], (KEY_VALUE_HEADS, CONTEXT_BLOCKS), jnp.float32) ** block_levels(key_of[4], (KEY_VALUE_HEADS, CONTEXT_BLOCKS), ((0, 4), (1, 8)), -0.2, 0.2)), 0.5, 2.0)
    selection = draw_selection(jax.random.fold_in(key_of[6], 71), 0)
    return {"queries": queries, "keys": keys, "values": values, "key_block_scale": key_block_scale, "value_block_scale": value_block_scale, "selection": selection}


def one_head(packed):
    query_group, key_head, value_head, key_scales, value_scales, chosen = packed
    key_rows = key_head.reshape(CONTEXT_BLOCKS, BLK, HEAD_SIZE)[chosen].reshape(SEL * BLK, HEAD_SIZE)
    value_rows = value_head.reshape(CONTEXT_BLOCKS, BLK, HEAD_SIZE)[chosen].reshape(SEL * BLK, HEAD_SIZE)
    key_factor = jnp.repeat(key_scales[chosen] * (1.0 / (HEAD_SIZE ** 0.5)), BLK, total_repeat_length=SEL * BLK)
    value_factor = jnp.repeat(value_scales[chosen], BLK, total_repeat_length=SEL * BLK)

    def one_query_head(query_rows):
        scores = jnp.dot(query_rows, key_rows.T, preferred_element_type=jnp.float32) * key_factor
        peak = jnp.max(scores, axis=1)
        prob = jnp.exp(scores - peak[:, None])
        total = jnp.sum(prob, axis=1)
        weights = (prob * value_factor).astype(jnp.bfloat16)
        summed = jnp.dot(weights, value_rows, preferred_element_type=jnp.float32)
        return summed / total[:, None]

    return lax.map(one_query_head, query_group)


def reference(queries, keys, values, key_block_scale, value_block_scale, selection):
    grouped_queries = queries.reshape(QUERY_TOKENS, KEY_VALUE_HEADS, QUERY_PER_KEY, HEAD_SIZE).transpose(1, 2, 0, 3)
    result = lax.map(one_head, (grouped_queries, keys, values, key_block_scale, value_block_scale, selection))
    return result.transpose(2, 0, 1, 3).reshape(QUERY_TOKENS, HQ, HEAD_SIZE).astype(jnp.bfloat16)
```

```python
import functools
import math

import jax
import jax.numpy as jnp
from jax import lax
from jax.experimental import pallas as pl
from jax.experimental.pallas import tpu as pltpu
from jax.sharding import PartitionSpec as P


MOST = 40
LANES = 128
PACK = 16
PARTS = 3
NEG = -1e30
SAFE = 2.0**64


def locate(sel_ref, g, bound):
    length = sel_ref.shape[1]

    def halve(_, span):
        low, high = span
        mid = (low + high) // 2
        below = jnp.logical_and(low < high, sel_ref[g, jnp.minimum(mid, length - 1)] < bound)
        rest = jnp.logical_or(below, low >= high)
        return jnp.where(below, mid + 1, low), jnp.where(rest, high, mid)

    span = (jnp.int32(0), jnp.int32(length))
    return lax.fori_loop(0, length.bit_length(), halve, span)[0]


def attend_kernel(cfg, base_ref, sel_ref, ks_ref, vs_ref, q_ref, k_hbm, v_hbm, *rest):
    heads, group, owners, block, per_tile, local = cfg
    msgs = rest[:owners]
    kbuf, vbuf, acc, m_scr, lse_scr, ksem, vsem = rest[owners:]
    tile_keys = per_tile * block
    width = k_hbm.shape[-1]
    rows = acc.shape[1]
    most_turns = kbuf.shape[1] // tile_keys - 1
    factor = math.log2(math.e) / math.sqrt(width)
    base = base_ref[0]

    spans = []
    for g in range(heads):
        first = locate(sel_ref, g, base)
        count = locate(sel_ref, g, base + local) - first
        turns = jnp.minimum((count + per_tile - 1) // per_tile, most_turns)
        spans.append((first, count, turns))

    def block_of(g, slot):
        first, count, _ = spans[g]
        return sel_ref[g, first + jnp.minimum(slot, count - 1)] - base

    def fetch(g, t):
        for b in range(per_tile):
            source = pl.ds(pl.multiple_of(block_of(g, t * per_tile + b) * block, block), block)
            target = pl.ds(pl.multiple_of(t * tile_keys + b * block, block), block)
            pltpu.make_async_copy(k_hbm.at[g, source], kbuf.at[g, target], ksem.at[g, t]).start()
            pltpu.make_async_copy(v_hbm.at[g, source], vbuf.at[g, target], vsem.at[g, t]).start()

    def arrive(g, t):
        at = pl.ds(pl.multiple_of(t * tile_keys, tile_keys), tile_keys)
        some = pl.ds(0, tile_keys)
        pltpu.make_async_copy(k_hbm.at[g, some], kbuf.at[g, at], ksem.at[g, t]).wait()
        pltpu.make_async_copy(v_hbm.at[g, some], vbuf.at[g, at], vsem.at[g, t]).wait()

    for g in range(heads):
        fetch(g, 0)

    for g in range(heads):
        count, turns = spans[g][1:]

        def tile(t, g=g, count=count):
            at = pl.ds(pl.multiple_of(t * tile_keys, tile_keys), tile_keys)
            kf, vf = [], []
            for b in range(per_tile):
                slot = t * per_tile + b
                kf.append(ks_ref[g, block_of(g, slot)] * factor)
                vf.append(jnp.where(slot < count, vs_ref[g, block_of(g, slot)], 0.0))
            v = vbuf[g, at, :].astype(jnp.float32)
            v = jnp.concatenate([v[b * block : (b + 1) * block] * vf[b] for b in range(per_tile)], axis=0)
            key_at = lax.broadcasted_iota(jnp.int32, (PACK, tile_keys), 1) + t * tile_keys
            live = jnp.where(key_at < count * block, 1.0, 0.0).astype(jnp.bfloat16)
            turned = jnp.concatenate([v.T.astype(jnp.bfloat16), live], axis=0)
            return kbuf[g, at, :], kf, turned

        query = q_ref[:, g * group : (g + 1) * group, :].reshape(rows, width)

        def score(k, query=query):
            return lax.dot_general(
                k, query, (((1,), (1,)), ((), ())), preferred_element_type=jnp.float32
            )

        def quick(t, _, g=g, tile=tile, score=score):
            fetch(g, t + 1)
            k, kf, turned = tile(t)
            s = score(k)
            m = m_scr[...]
            weights = [
                jnp.exp2(s[b * block : (b + 1) * block] * kf[b] - m).astype(jnp.bfloat16)
                for b in range(per_tile)
            ]
            acc[...] += jnp.dot(
                turned, jnp.concatenate(weights, axis=0), preferred_element_type=jnp.float32
            )
            arrive(g, t + 1)
            return 0

        def careful(t, _, tile=tile, score=score):
            k, kf, turned = tile(t)
            s = score(k)
            s = [s[b * block : (b + 1) * block] * kf[b] for b in range(per_tile)]
            old = m_scr[...]
            new = jnp.maximum(old, jnp.max(functools.reduce(jnp.maximum, s), axis=0, keepdims=True))
            weights = jnp.concatenate([jnp.exp2(x - new).astype(jnp.bfloat16) for x in s], axis=0)
            acc[...] = acc[...] * jnp.exp2(old - new) + jnp.dot(
                turned, weights, preferred_element_type=jnp.float32
            )
            m_scr[...] = new
            return 0

        acc[...] = jnp.zeros_like(acc)
        arrive(g, 0)
        m_scr[...] = jnp.max(score(kbuf[g, 0:block, :]), axis=0, keepdims=True) * (
            ks_ref[g, block_of(g, 0)] * factor
        )
        lax.fori_loop(0, turns, quick, 0)

        @pl.when(jnp.logical_not(jnp.max(acc[width : width + 1, :]) < SAFE))
        def _(turns=turns, careful=careful):
            acc[...] = jnp.zeros_like(acc)
            m_scr[...] = jnp.full_like(m_scr, NEG)
            lax.fori_loop(0, turns, careful, 0)

        blocks = rows // owners // LANES
        for x in range(owners):
            for b in range(blocks):
                at = pl.ds((x * blocks + b) * LANES, LANES)
                j = g * blocks + b
                total = acc[width : width + 1, at]
                msgs[x][j * width : (j + 1) * width, :] = (acc[:width, at] / total).astype(jnp.bfloat16)
                lse_scr[x, j : j + 1, :] = m_scr[:, at] + jnp.log2(total)

    for x in range(owners):
        put_level(msgs[x], lse_scr[x], heads * (rows // owners // LANES) * width)


def put_level(msg_ref, level, at):
    for i in range(PARTS):
        part = level.astype(jnp.bfloat16)
        msg_ref[at + i * PACK : at + i * PACK + level.shape[0], :] = part
        level = level - part.astype(jnp.float32)


def get_level(msg_ref, n, at):
    parts = [msg_ref[at + i * PACK : at + i * PACK + n, :].astype(jnp.float32) for i in range(PARTS)]
    return functools.reduce(jnp.add, parts)


def merge_weights(refs, n, at):
    levels = [get_level(ref, n, at) for ref in refs]
    peak = functools.reduce(jnp.maximum, levels)
    shares = [jnp.exp2(level - peak) for level in levels]
    whole = functools.reduce(jnp.add, shares)
    return [share / whole for share in shares], peak + jnp.log2(whole)


def merge_kernel(n, width, *refs):
    out = refs[-1]
    ins = refs[:-1]
    level_rows = max(8, n)
    shares, level = merge_weights(ins, level_rows, n * width)
    for j in range(n):
        at = pl.ds(j * width, width)
        values = [ref[at, :].astype(jnp.float32) * share[j : j + 1] for ref, share in zip(ins, shares)]
        out[at, :] = functools.reduce(jnp.add, values).astype(jnp.bfloat16)
    put_level(out, level, n * width)


def merge(msgs, n, width):
    return pl.pallas_call(
        functools.partial(merge_kernel, n, width),
        out_shape=jax.ShapeDtypeStruct(msgs[0].shape, msgs[0].dtype),
        in_specs=[pl.BlockSpec(memory_space=pltpu.VMEM)] * len(msgs),
        out_specs=pl.BlockSpec(memory_space=pltpu.VMEM),
        cost_estimate=pl.CostEstimate(flops=msgs[0].size * 4, bytes_accessed=msgs[0].size * 6, transcendentals=0),
    )(*msgs)


def finish_kernel(cfg, pick_ref, *refs):
    heads, group, n, width, stages = cfg
    pairs, out, mine, theirs, sems = refs[: 2 * stages], refs[-4], refs[-3], refs[-2], refs[-1]
    for k in range(stages):

        @pl.when(pick_ref[0] == k)
        def _(k=k):
            first = pltpu.make_async_copy(pairs[2 * k], mine, sems.at[0])
            second = pltpu.make_async_copy(pairs[2 * k + 1], theirs, sems.at[1])
            first.start()
            second.start()
            first.wait()
            second.wait()

    shares, _ = merge_weights([mine, theirs], max(8, n), n * width)
    blocks = n // heads
    tokens = LANES // group
    for g in range(heads):
        for b in range(blocks):
            j = g * blocks + b
            at = pl.ds(j * width, width)
            value = mine[at, :].astype(jnp.float32) * shares[0][j : j + 1]
            value += theirs[at, :].astype(jnp.float32) * shares[1][j : j + 1]
            turned = value.T.astype(jnp.bfloat16).reshape(tokens, group, width)
            out[b * tokens : (b + 1) * tokens, g * group : (g + 1) * group, :] = turned


def finish(pick, pairs, heads, group, n, width):
    stages = len(pairs) // 2
    tokens = n // heads * LANES // group
    shape = pairs[0].shape
    return pl.pallas_call(
        functools.partial(finish_kernel, (heads, group, n, width, stages)),
        out_shape=jax.ShapeDtypeStruct((tokens, heads * group, width), jnp.bfloat16),
        in_specs=[pl.BlockSpec(memory_space=pltpu.SMEM)] + [pl.BlockSpec(memory_space=pl.ANY)] * len(pairs),
        out_specs=pl.BlockSpec(memory_space=pltpu.VMEM),
        scratch_shapes=[
            pltpu.VMEM(shape, jnp.bfloat16),
            pltpu.VMEM(shape, jnp.bfloat16),
            pltpu.SemaphoreType.DMA((2,)),
        ],
    )(pick, *pairs)


def attend(q, k, v, key_scale, value_scale, selection, base, owners, per_tile=8):
    heads, _, width = k.shape
    local = key_scale.shape[1]
    block = k.shape[1] // local
    group = q.shape[1] // heads
    rows = q.shape[0] * group
    n = heads * (rows // owners // LANES)
    turns = -(-min(MOST, local) // per_tile)
    keys = (turns + 1) * per_tile * block
    smem = pl.BlockSpec(memory_space=pltpu.SMEM)
    vmem = pl.BlockSpec(memory_space=pltpu.VMEM)
    hbm = pl.BlockSpec(memory_space=pl.ANY)
    message = jax.ShapeDtypeStruct((n * width + PARTS * PACK, LANES), jnp.bfloat16)
    likely = heads * rows * selection.shape[1] * block * local // (selection.shape[1] * 4)
    return pl.pallas_call(
        functools.partial(attend_kernel, (heads, group, owners, block, per_tile, local)),
        out_shape=[message] * owners,
        in_specs=[smem, smem, smem, smem, vmem, hbm, hbm],
        out_specs=[vmem] * owners,
        scratch_shapes=[
            pltpu.VMEM((heads, keys, width), jnp.bfloat16),
            pltpu.VMEM((heads, keys, width), jnp.bfloat16),
            pltpu.VMEM((width + PACK, rows), jnp.float32),
            pltpu.VMEM((1, rows), jnp.float32),
            pltpu.VMEM((owners, max(8, n), LANES), jnp.float32),
            pltpu.SemaphoreType.DMA((heads, turns + 1)),
            pltpu.SemaphoreType.DMA((heads, turns + 1)),
        ],
        compiler_params=pltpu.CompilerParams(vmem_limit_bytes=32 << 20),
        cost_estimate=pl.CostEstimate(flops=4 * likely * width, bytes_accessed=4 << 20, transcendentals=likely),
    )(base, selection, key_scale, value_scale, q, k, v)


def on_device(ctx_size, head_size, queries, keys, values, key_block_scale, value_block_scale, selection):
    heads, _, width = keys.shape
    local = key_block_scale.shape[1]
    mine = queries.shape[1] // head_size
    group = mine // heads
    owners = ctx_size // head_size
    ctx = lax.axis_index("ctx")
    head = lax.axis_index("head")
    place, owner = ctx // owners, ctx % owners
    base = (ctx * local).astype(jnp.int32).reshape(1)
    blocks = queries.shape[0] * group // owners // LANES
    n = heads * blocks

    def part(k):
        return lax.dynamic_slice_in_dim(queries, (head ^ k) * mine, mine, axis=1)

    def swap(x, k):
        return lax.ppermute(x, "head", [(i, i ^ k) for i in range(head_size)])

    chunks = [part(0)] + [swap(part(k), k) for k in range(1, head_size)]

    def index(c, h):
        return c * head_size + h

    pairs = []
    for k in range(head_size):
        msgs = attend(chunks[k], keys, values, key_block_scale, value_block_scale, selection, base, owners)
        stacked = jnp.stack(msgs) if owners > 2 else None

        def kept(d):
            if owners == 2:
                return jnp.where((owner ^ d) == 0, msgs[0], msgs[1])
            return lax.dynamic_index_in_dim(stacked, owner ^ d, 0, keepdims=False)

        gathered = [kept(0)] + [
            lax.ppermute(kept(d), "ctx", [(c, c ^ d) for c in range(ctx_size)]) for d in range(1, owners)
        ]
        held = merge(gathered, n, width)
        bits = head_size.bit_length() - 1
        for bit in range(bits):
            step = 1 << bit
            routes = []
            for c in range(ctx_size):
                for h in range(head_size):
                    apart = (c // owners) ^ h ^ k
                    if apart & (2 * step - 1) == step:
                        routes.append((index(c, h), index(c ^ (step * owners), h)))
            got = lax.ppermute(held, ("ctx", "head"), routes)
            if bit < bits - 1:
                held = merge([held, got], n, width)
        pairs += [held, got]
    pick = (place ^ head).astype(jnp.int32).reshape(1)
    return finish(pick, pairs, heads, group, n, width)


def solution(mesh):
    return jax.shard_map(
        functools.partial(on_device, mesh.shape["ctx"], mesh.shape["head"]),
        mesh=mesh,
        in_specs=(
            P("head", None, None),
            P("head", "ctx", None),
            P("head", "ctx", None),
            P("head", "ctx"),
            P("head", "ctx"),
            P("head", None),
        ),
        out_specs=P("ctx", "head", None),
        check_vma=False,
    )
```

```python
import functools
import math

import jax
import jax.numpy as jnp
from jax import lax
from jax.experimental import pallas as pl
from jax.experimental.pallas import tpu as pltpu
from jax.sharding import PartitionSpec as P


MOST = 40
LANES = 128
PACK = 16
PARTS = 3
PER_TILE = 8
NEG = -1e30
SAFE = 2.0**64

SMEM = pl.BlockSpec(memory_space=pltpu.SMEM)
VMEM = pl.BlockSpec(memory_space=pltpu.VMEM)
HBM = pl.BlockSpec(memory_space=pltpu.HBM)


def locate(sel_ref, g, bound):
    length = sel_ref.shape[1]

    def halve(_, span):
        low, high = span
        mid = (low + high) // 2
        below = jnp.logical_and(low < high, sel_ref[g, jnp.minimum(mid, length - 1)] < bound)
        rest = jnp.logical_or(below, low >= high)
        return jnp.where(below, mid + 1, low), jnp.where(rest, high, mid)

    span = (jnp.int32(0), jnp.int32(length))
    return lax.fori_loop(0, length.bit_length(), halve, span)[0]


def collect_kernel(block, local, where_ref, sel_ref, ks_ref, vs_ref, k_hbm, v_hbm, tiles, table, scales, vbuf, ksem, vsem):
    heads, _, width = k_hbm.shape
    most = (tiles.shape[0]) // heads
    keys = PER_TILE * block
    factor = math.log2(math.e) / math.sqrt(width)
    base = where_ref[0]
    spans = []
    start = jnp.int32(0)
    for g in range(heads):
        first = locate(sel_ref, g, base)
        count = locate(sel_ref, g, base + local) - first
        turns = jnp.minimum((count + PER_TILE - 1) // PER_TILE, most)
        table[g] = start
        spans.append((first, count, turns, start))
        start = start + turns
    table[heads] = start

    for g in range(heads):
        first, count, turns, start = spans[g]

        def fetch(t, _, g=g, first=first, count=count, start=start):
            i = start + t
            for b in range(PER_TILE):
                slot = t * PER_TILE + b
                at = sel_ref[g, first + jnp.minimum(slot, count - 1)] - base
                source = pl.ds(pl.multiple_of(at * block, block), block)
                target = pl.ds(b * block, block)
                pltpu.make_async_copy(v_hbm.at[g, source], vbuf.at[i, target], vsem.at[i]).start()
                pltpu.make_async_copy(k_hbm.at[g, source], tiles.at[i, target], ksem.at[i]).start()
                scales[i, b] = ks_ref[g, at] * factor
            return 0

        lax.fori_loop(0, turns, fetch, 0)

    for g in range(heads):
        first, count, turns, start = spans[g]

        def turn(t, _, g=g, first=first, count=count, start=start):
            i = start + t
            some = pl.ds(0, keys)
            pltpu.make_async_copy(v_hbm.at[g, some], vbuf.at[i], vsem.at[i]).wait()
            for b in range(0, PER_TILE, LANES // block):
                rows = []
                for c in range(b, b + LANES // block):
                    slot = t * PER_TILE + c
                    at = sel_ref[g, first + jnp.minimum(slot, count - 1)] - base
                    scale = jnp.where(slot < count, vs_ref[g, at], 0.0)
                    rows.append(vbuf[i, c * block : (c + 1) * block, :].astype(jnp.float32) * scale)
                key_at = lax.broadcasted_iota(jnp.int32, (PACK, LANES), 1) + (t * keys + b * block)
                live = jnp.where(key_at < count * block, 1.0, 0.0).astype(jnp.bfloat16)
                at = keys + b * block // LANES * (width + PACK)
                tiles[i, at : at + width, :] = jnp.concatenate(rows, axis=0).T.astype(jnp.bfloat16)
                tiles[i, at + width : at + width + PACK, :] = live
            pltpu.make_async_copy(k_hbm.at[g, some], tiles.at[i, some], ksem.at[i]).wait()
            return 0

        lax.fori_loop(0, turns, turn, 0)


def collect(where, selection, key_scale, value_scale, k, v):
    heads, _, width = k.shape
    local = key_scale.shape[1]
    block = k.shape[1] // local
    keys = PER_TILE * block
    most = -(-min(MOST, local) // PER_TILE) * heads
    height = keys + keys // LANES * (width + PACK)
    return pl.pallas_call(
        functools.partial(collect_kernel, block, local),
        out_shape=[
            jax.ShapeDtypeStruct((most, height, width), jnp.bfloat16),
            jax.ShapeDtypeStruct((heads + 1,), jnp.int32),
            jax.ShapeDtypeStruct((most, PER_TILE), jnp.float32),
        ],
        in_specs=[SMEM, SMEM, SMEM, SMEM, HBM, HBM],
        out_specs=[VMEM, SMEM, SMEM],
        scratch_shapes=[
            pltpu.VMEM((most, keys, width), jnp.bfloat16),
            pltpu.SemaphoreType.DMA((most,)),
            pltpu.SemaphoreType.DMA((most,)),
        ],
        compiler_params=pltpu.CompilerParams(vmem_limit_bytes=58 << 20),
        cost_estimate=pl.CostEstimate(flops=0, bytes_accessed=6 << 20, transcendentals=0),
    )(where, selection, key_scale, value_scale, k, v)


def attend_kernel(cfg, where_ref, table, scales, q_ref, tiles, *rest):
    heads, group, owners, block = cfg
    msgs = rest[:owners]
    acc, m_scr, lse_scr = rest[owners:]
    keys = PER_TILE * block
    width = tiles.shape[-1]
    rows = acc.shape[2]
    low, high = table[heads[0]], table[heads[-1] + 1]

    def query(g):
        return q_ref[:, pl.ds(pl.multiple_of(g * group, group), group), :].reshape(rows, width)

    def score(k, q):
        return lax.dot_general(k, q, (((1,), (1,)), ((), ())), preferred_element_type=jnp.float32)

    def head_of(i):
        g = jnp.int32(heads[0])
        for h in heads[1:]:
            g = g + (i >= table[h]).astype(jnp.int32)
        return g

    def scaled(i, q):
        s = score(tiles[i, :keys, :], q)
        return [s[b * block : (b + 1) * block] * scales[i, b] for b in range(PER_TILE)]

    def values(i):
        step = width + PACK
        parts = [tiles[i, keys + c * step : keys + (c + 1) * step, :] for c in range(keys // LANES)]
        return jnp.concatenate(parts, axis=1)

    def quick(i, _):
        g = head_of(i)
        at = g - heads[0]
        m = m_scr[at]
        weights = [jnp.exp2(x - m).astype(jnp.bfloat16) for x in scaled(i, query(g))]
        acc[at] += jnp.dot(values(i), jnp.concatenate(weights, axis=0), preferred_element_type=jnp.float32)
        return 0

    def careful(i, _):
        g = head_of(i)
        at = g - heads[0]
        s = scaled(i, query(g))
        old = m_scr[at]
        new = jnp.maximum(old, jnp.max(functools.reduce(jnp.maximum, s), axis=0, keepdims=True))
        weights = jnp.concatenate([jnp.exp2(x - new).astype(jnp.bfloat16) for x in s], axis=0)
        acc[at] = acc[at] * jnp.exp2(old - new) + jnp.dot(
            values(i), weights, preferred_element_type=jnp.float32
        )
        m_scr[at] = new
        return 0

    acc[...] = jnp.zeros_like(acc)
    for n, g in enumerate(heads):
        first = table[g]
        q = q_ref[:, g * group : (g + 1) * group, :].reshape(rows, width)
        m_scr[n] = jnp.max(score(tiles[first, :block, :], q), axis=0, keepdims=True) * scales[first, 0]
    lax.fori_loop(low, high, quick, 0)

    @pl.when(jnp.logical_not(jnp.max(acc[:, width : width + 1, :]) < SAFE))
    def _():
        acc[...] = jnp.zeros_like(acc)
        m_scr[...] = jnp.full_like(m_scr, NEG)
        lax.fori_loop(low, high, careful, 0)

    blocks = rows // owners // LANES
    size = section(blocks, width)
    for d in range(owners):
        x = where_ref[1] ^ d
        for n in range(len(heads)):
            for b in range(blocks):
                at = pl.ds(pl.multiple_of((x * blocks + b) * LANES, LANES), LANES)
                total = acc[n, width : width + 1, at]
                row = n * size + b * width
                msgs[d][row : row + width, :] = (acc[n, :width, at] / total).astype(jnp.bfloat16)
                lse_scr[b : b + 1, :] = m_scr[n, :, at] + jnp.log2(total)
            put_level(msgs[d], lse_scr[...], n * size + blocks * width)


def section(blocks, width):
    return blocks * width + PARTS * PACK


def put_level(msg_ref, level, at):
    for i in range(PARTS):
        part = level.astype(jnp.bfloat16)
        msg_ref[at + i * PACK : at + i * PACK + level.shape[0], :] = part
        level = level - part.astype(jnp.float32)


def get_level(msg_ref, at):
    parts = [msg_ref[at + i * PACK : at + i * PACK + 8, :].astype(jnp.float32) for i in range(PARTS)]
    return functools.reduce(jnp.add, parts)


def merge_weights(refs, at):
    levels = [get_level(ref, at) for ref in refs]
    peak = functools.reduce(jnp.maximum, levels)
    shares = [jnp.exp2(level - peak) for level in levels]
    whole = functools.reduce(jnp.add, shares)
    return [share / whole for share in shares], peak + jnp.log2(whole)


def merged(refs, shares, row, b, width):
    values = [ref[row : row + width, :].astype(jnp.float32) * share[b : b + 1] for ref, share in zip(refs, shares)]
    return functools.reduce(jnp.add, values)


def merge_kernel(blocks, width, *refs):
    out = refs[-1]
    ins = refs[:-1]
    size = section(blocks, width)
    for n in range(out.shape[0] // size):
        shares, level = merge_weights(ins, n * size + blocks * width)
        for b in range(blocks):
            row = n * size + b * width
            out[row : row + width, :] = merged(ins, shares, row, b, width).astype(jnp.bfloat16)
        put_level(out, level, n * size + blocks * width)


def merge(msgs, blocks, width):
    return pl.pallas_call(
        functools.partial(merge_kernel, blocks, width),
        out_shape=jax.ShapeDtypeStruct(msgs[0].shape, msgs[0].dtype),
        in_specs=[VMEM] * len(msgs),
        out_specs=VMEM,
        compiler_params=pltpu.CompilerParams(vmem_limit_bytes=4 << 20),
        cost_estimate=pl.CostEstimate(flops=msgs[0].size * 4, bytes_accessed=msgs[0].size * 6, transcendentals=0),
    )(*msgs)


def finish_kernel(units, group, blocks, width, pick_ref, *refs):
    out, held, sems = refs[-3:]
    size = section(blocks, width)
    stages = 1 + max(k for k, _, _ in units)
    for stage in range(stages):

        @pl.when(pick_ref[0] == stage)
        def _(stage=stage):
            at = 0
            copies = []
            for k, heads, many in units:
                if k == stage:
                    for n, g in enumerate(heads):
                        for i in range(many):
                            source = refs[at + i].at[pl.ds(n * size, size)]
                            copies.append(pltpu.make_async_copy(source, held.at[g, i], sems.at[g, i]))
                at += many
            for copy in copies:
                copy.start()
            for copy in copies:
                copy.wait()

    tokens = LANES // group
    for g in range(held.shape[0]):
        ins = [held.at[g, i] for i in range(held.shape[1])]
        shares, _ = merge_weights(ins, blocks * width)
        for b in range(blocks):
            value = merged(ins, shares, b * width, b, width)
            turned = value.T.astype(jnp.bfloat16).reshape(tokens, group, width)
            out[b * tokens : (b + 1) * tokens, g * group : (g + 1) * group, :] = turned


def finish(pick, units, heads, group, blocks, width):
    many = len(units[0][2])
    msgs = [msg for _, _, msgs in units for msg in msgs]
    shape = tuple((k, hs, len(ms)) for k, hs, ms in units)
    return pl.pallas_call(
        functools.partial(finish_kernel, shape, group, blocks, width),
        out_shape=jax.ShapeDtypeStruct((blocks * LANES // group, heads * group, width), jnp.bfloat16),
        in_specs=[SMEM] + [HBM] * len(msgs),
        out_specs=VMEM,
        scratch_shapes=[
            pltpu.VMEM((heads, many, section(blocks, width), width), jnp.bfloat16),
            pltpu.SemaphoreType.DMA((heads, many)),
        ],
        compiler_params=pltpu.CompilerParams(vmem_limit_bytes=8 << 20),
    )(pick, *msgs)


def attend(where, table, scales, q, tiles, heads, group, owners, block):
    width = q.shape[2]
    rows = q.shape[0] * group
    blocks = rows // owners // LANES
    message = jax.ShapeDtypeStruct((len(heads) * section(blocks, width), width), jnp.bfloat16)
    likely = len(heads) * rows * 3 * PER_TILE * block
    return pl.pallas_call(
        functools.partial(attend_kernel, (heads, group, owners, block)),
        out_shape=[message] * owners,
        in_specs=[SMEM, SMEM, SMEM, VMEM, VMEM],
        out_specs=[VMEM] * owners,
        scratch_shapes=[
            pltpu.VMEM((len(heads), width + PACK, rows), jnp.float32),
            pltpu.VMEM((len(heads), 1, rows), jnp.float32),
            pltpu.VMEM((8, LANES), jnp.float32),
        ],
        compiler_params=pltpu.CompilerParams(vmem_limit_bytes=16 << 20),
        cost_estimate=pl.CostEstimate(flops=4 * likely * width, bytes_accessed=4 << 20, transcendentals=likely),
    )(where, table, scales, q, tiles)


def plan_units(head_size, heads):
    units = [(k, tuple(range(heads))) for k in range(head_size - 1)]
    return units + [(head_size - 1, (g,)) for g in range(heads)]


def on_device(ctx_size, head_size, queries, keys, values, key_block_scale, value_block_scale, selection):
    heads, _, width = keys.shape
    local = key_block_scale.shape[1]
    block = keys.shape[1] // local
    mine = queries.shape[1] // head_size
    group = mine // heads
    owners = ctx_size // head_size
    ctx = lax.axis_index("ctx")
    head = lax.axis_index("head")
    place, owner = ctx // owners, ctx % owners
    where = jnp.stack([ctx * local, owner]).astype(jnp.int32)
    blocks = queries.shape[0] * group // owners // LANES

    def part(k):
        return lax.dynamic_slice_in_dim(queries, (head ^ k) * mine, mine, axis=1)

    def swap(k):
        return lax.ppermute(part(k), "head", [(i, i ^ k) for i in range(head_size)])

    chunks = [part(0)] + [swap(k) for k in range(1, head_size)]
    tiles, table, scales = collect(where, selection, key_block_scale, value_block_scale, keys, values)

    def index(c, h):
        return c * head_size + h

    units = []
    for k, hs in plan_units(head_size, heads):
        msgs = attend(where, table, scales, chunks[k], tiles, hs, group, owners, block)
        got = [
            lax.ppermute(msgs[d], "ctx", [(c, c ^ d) for c in range(ctx_size)]) for d in range(1, owners)
        ]
        held = merge([msgs[0]] + got, blocks, width)
        far = [held]
        for apart in range(1, head_size):
            routes = []
            for c in range(ctx_size):
                for h in range(head_size):
                    if (c // owners) ^ h ^ k == apart:
                        routes.append((index(c, h), index(c ^ (apart * owners), h)))
            far.append(lax.ppermute(held, ("ctx", "head"), routes))
        units.append((k, hs, far))
    pick = (place ^ head).astype(jnp.int32).reshape(1)
    return finish(pick, units, heads, group, blocks, width)


def solution(mesh):
    ctx_size, head_size = mesh.shape["ctx"], mesh.shape["head"]

    def body(*args):
        return on_device(ctx_size, head_size, *args)

    return jax.shard_map(
        body,
        mesh=mesh,
        in_specs=(
            P("head", None, None),
            P("head", "ctx", None),
            P("head", "ctx", None),
            P("head", "ctx"),
            P("head", "ctx"),
            P("head", None),
        ),
        out_specs=P("ctx", "head", None),
        check_vma=False,
    )
```

```python
import functools
import math

import jax
import jax.numpy as jnp
from jax import lax
from jax.experimental import pallas as pl
from jax.experimental.pallas import tpu as pltpu
from jax.sharding import PartitionSpec as P


MOST = 40
LANES = 128
PACK = 16
PARTS = 3
PER_TILE = 8
NEG = -1e30
SAFE = 2.0**64

SMEM = pl.BlockSpec(memory_space=pltpu.SMEM)
VMEM = pl.BlockSpec(memory_space=pltpu.VMEM)
HBM = pl.BlockSpec(memory_space=pltpu.HBM)


def keep_out(x):
    return pltpu.with_memory_space_constraint(x, pltpu.HBM)


def locate(sel_ref, g, bound):
    length = sel_ref.shape[1]

    def halve(_, span):
        low, high = span
        mid = (low + high) // 2
        below = jnp.logical_and(low < high, sel_ref[g, jnp.minimum(mid, length - 1)] < bound)
        rest = jnp.logical_or(below, low >= high)
        return jnp.where(below, mid + 1, low), jnp.where(rest, high, mid)

    span = (jnp.int32(0), jnp.int32(length))
    return lax.fori_loop(0, length.bit_length(), halve, span)[0]


def collect_kernel(block, local, sel_ref, ks_ref, vs_ref, k_hbm, v_hbm, tiles, table, scales, vbuf, ksem, vsem):
    heads, _, width = k_hbm.shape
    most = (tiles.shape[0]) // heads
    keys = PER_TILE * block
    factor = math.log2(math.e) / math.sqrt(width)
    base = lax.axis_index("ctx") * local
    spans = []
    start = jnp.int32(0)
    for g in range(heads):
        first = locate(sel_ref, g, base)
        count = locate(sel_ref, g, base + local) - first
        turns = jnp.minimum((count + PER_TILE - 1) // PER_TILE, most)
        table[g] = start
        spans.append((first, count, turns, start))
        start = start + turns
    table[heads] = start

    for g in range(heads):
        first, count, turns, start = spans[g]

        def fetch(t, _, g=g, first=first, count=count, start=start):
            i = start + t
            for b in range(PER_TILE):
                slot = t * PER_TILE + b
                at = sel_ref[g, first + jnp.minimum(slot, count - 1)] - base
                source = pl.ds(pl.multiple_of(at * block, block), block)
                target = pl.ds(b * block, block)
                pltpu.make_async_copy(v_hbm.at[g, source], vbuf.at[i, target], vsem.at[i]).start()
                pltpu.make_async_copy(k_hbm.at[g, source], tiles.at[i, target], ksem.at[i]).start()
                scales[i, b] = ks_ref[g, at] * factor
            return 0

        lax.fori_loop(0, turns, fetch, 0)

    for g in range(heads):
        first, count, turns, start = spans[g]

        def turn(t, _, g=g, first=first, count=count, start=start):
            i = start + t
            some = pl.ds(0, keys)
            pltpu.make_async_copy(v_hbm.at[g, some], vbuf.at[i], vsem.at[i]).wait()
            for b in range(0, PER_TILE, LANES // block):
                rows = []
                for c in range(b, b + LANES // block):
                    slot = t * PER_TILE + c
                    at = sel_ref[g, first + jnp.minimum(slot, count - 1)] - base
                    scale = jnp.where(slot < count, vs_ref[g, at], 0.0)
                    rows.append(vbuf[i, c * block : (c + 1) * block, :].astype(jnp.float32) * scale)
                key_at = lax.broadcasted_iota(jnp.int32, (PACK, LANES), 1) + (t * keys + b * block)
                live = jnp.where(key_at < count * block, 1.0, 0.0).astype(jnp.bfloat16)
                at = keys + b * block // LANES * (width + PACK)
                tiles[i, at : at + width, :] = jnp.concatenate(rows, axis=0).T.astype(jnp.bfloat16)
                tiles[i, at + width : at + width + PACK, :] = live
            pltpu.make_async_copy(k_hbm.at[g, some], tiles.at[i, some], ksem.at[i]).wait()
            return 0

        lax.fori_loop(0, turns, turn, 0)


def collect(selection, key_scale, value_scale, k, v):
    heads, _, width = k.shape
    local = key_scale.shape[1]
    block = k.shape[1] // local
    keys = PER_TILE * block
    most = -(-min(MOST, local) // PER_TILE) * heads
    height = keys + keys // LANES * (width + PACK)
    return pl.pallas_call(
        functools.partial(collect_kernel, block, local),
        out_shape=[
            jax.ShapeDtypeStruct((most, height, width), jnp.bfloat16),
            jax.ShapeDtypeStruct((heads + 1,), jnp.int32),
            jax.ShapeDtypeStruct((most, PER_TILE), jnp.float32),
        ],
        in_specs=[SMEM, SMEM, SMEM, HBM, HBM],
        out_specs=[VMEM, SMEM, SMEM],
        scratch_shapes=[
            pltpu.VMEM((most, keys, width), jnp.bfloat16),
            pltpu.SemaphoreType.DMA((most,)),
            pltpu.SemaphoreType.DMA((most,)),
        ],
        compiler_params=pltpu.CompilerParams(vmem_limit_bytes=16 << 20),
        cost_estimate=pl.CostEstimate(flops=0, bytes_accessed=6 << 20, transcendentals=0),
    )(selection, key_scale, value_scale, k, v)


def attend_kernel(cfg, table, scales, q_ref, tiles, *rest):
    heads, group, owners, block = cfg
    msgs = rest[:owners]
    acc, m_scr, lse_scr = rest[owners:]
    keys = PER_TILE * block
    width = tiles.shape[-1]
    rows = acc.shape[2]
    low, high = table[heads[0]], table[heads[-1] + 1]

    def query(g):
        return q_ref[:, pl.ds(pl.multiple_of(g * group, group), group), :].reshape(rows, width)

    def score(k, q):
        return lax.dot_general(k, q, (((1,), (1,)), ((), ())), preferred_element_type=jnp.float32)

    def head_of(i):
        g = jnp.int32(heads[0])
        for h in heads[1:]:
            g = g + (i >= table[h]).astype(jnp.int32)
        return g

    def scaled(i, q):
        s = score(tiles[i, :keys, :], q)
        return [s[b * block : (b + 1) * block] * scales[i, b] for b in range(PER_TILE)]

    def values(i):
        step = width + PACK
        parts = [tiles[i, keys + c * step : keys + (c + 1) * step, :] for c in range(keys // LANES)]
        return jnp.concatenate(parts, axis=1)

    def quick(i, _):
        g = head_of(i)
        at = g - heads[0]
        m = m_scr[at]
        weights = [jnp.exp2(x - m).astype(jnp.bfloat16) for x in scaled(i, query(g))]
        acc[at] += jnp.dot(values(i), jnp.concatenate(weights, axis=0), preferred_element_type=jnp.float32)
        return 0

    def careful(i, _):
        g = head_of(i)
        at = g - heads[0]
        s = scaled(i, query(g))
        old = m_scr[at]
        new = jnp.maximum(old, jnp.max(functools.reduce(jnp.maximum, s), axis=0, keepdims=True))
        weights = jnp.concatenate([jnp.exp2(x - new).astype(jnp.bfloat16) for x in s], axis=0)
        acc[at] = acc[at] * jnp.exp2(old - new) + jnp.dot(
            values(i), weights, preferred_element_type=jnp.float32
        )
        m_scr[at] = new
        return 0

    acc[...] = jnp.zeros_like(acc)
    for n, g in enumerate(heads):
        first = table[g]
        q = q_ref[:, g * group : (g + 1) * group, :].reshape(rows, width)
        m_scr[n] = jnp.max(score(tiles[first, :block, :], q), axis=0, keepdims=True) * scales[first, 0]
    lax.fori_loop(low, high, quick, 0)

    @pl.when(jnp.logical_not(jnp.max(acc[:, width : width + 1, :]) < SAFE))
    def _():
        acc[...] = jnp.zeros_like(acc)
        m_scr[...] = jnp.full_like(m_scr, NEG)
        lax.fori_loop(low, high, careful, 0)

    blocks = rows // owners // LANES
    size = section(blocks, width)
    for d in range(owners):
        x = lax.rem(lax.axis_index("ctx"), owners) ^ d
        for n in range(len(heads)):
            for b in range(blocks):
                at = pl.ds(pl.multiple_of((x * blocks + b) * LANES, LANES), LANES)
                total = acc[n, width : width + 1, at]
                row = n * size + b * width
                msgs[d][row : row + width, :] = (acc[n, :width, at] / total).astype(jnp.bfloat16)
                lse_scr[b : b + 1, :] = m_scr[n, :, at] + jnp.log2(total)
            put_level(msgs[d], lse_scr[...], n * size + blocks * width)


def section(blocks, width):
    return blocks * width + PARTS * PACK


def put_level(msg_ref, level, at):
    for i in range(PARTS):
        part = level.astype(jnp.bfloat16)
        msg_ref[at + i * PACK : at + i * PACK + level.shape[0], :] = part
        level = level - part.astype(jnp.float32)


def get_level(msg_ref, at):
    parts = [msg_ref[at + i * PACK : at + i * PACK + 8, :].astype(jnp.float32) for i in range(PARTS)]
    return functools.reduce(jnp.add, parts)


def merge_weights(refs, at):
    levels = [get_level(ref, at) for ref in refs]
    peak = functools.reduce(jnp.maximum, levels)
    shares = [jnp.exp2(level - peak) for level in levels]
    whole = functools.reduce(jnp.add, shares)
    return [share / whole for share in shares], peak + jnp.log2(whole)


def merged(refs, shares, row, b, width):
    values = [ref[row : row + width, :].astype(jnp.float32) * share[b : b + 1] for ref, share in zip(refs, shares)]
    return functools.reduce(jnp.add, values)


def merge_kernel(blocks, width, *refs):
    out = refs[-1]
    ins = refs[:-1]
    size = section(blocks, width)
    for n in range(out.shape[0] // size):
        shares, level = merge_weights(ins, n * size + blocks * width)
        for b in range(blocks):
            row = n * size + b * width
            out[row : row + width, :] = merged(ins, shares, row, b, width).astype(jnp.bfloat16)
        put_level(out, level, n * size + blocks * width)


def merge(msgs, blocks, width):
    return pl.pallas_call(
        functools.partial(merge_kernel, blocks, width),
        out_shape=jax.ShapeDtypeStruct(msgs[0].shape, msgs[0].dtype),
        in_specs=[VMEM] * len(msgs),
        out_specs=VMEM,
        compiler_params=pltpu.CompilerParams(vmem_limit_bytes=4 << 20),
        cost_estimate=pl.CostEstimate(flops=msgs[0].size * 4, bytes_accessed=msgs[0].size * 6, transcendentals=0),
    )(*msgs)


def part_kernel(group, q_hbm, *refs):
    chunks, sems = refs[:-1], refs[-1]
    copies = []
    for k, chunk in enumerate(chunks):
        at = pl.multiple_of((lax.axis_index("head") ^ k) * group, group)
        copies.append(pltpu.make_async_copy(q_hbm.at[:, pl.ds(at, group), :], chunk, sems.at[k]))
    for copy in copies:
        copy.start()
    for copy in copies:
        copy.wait()


def part(queries, many):
    tokens, heads, width = queries.shape
    return pl.pallas_call(
        functools.partial(part_kernel, heads // many),
        out_shape=[jax.ShapeDtypeStruct((tokens, heads // many, width), queries.dtype)] * many,
        in_specs=[HBM],
        out_specs=[VMEM] * many,
        scratch_shapes=[pltpu.SemaphoreType.DMA((many,))],
        compiler_params=pltpu.CompilerParams(vmem_limit_bytes=16 << 20),
    )(queries)


def pair_kernel(blocks, width, owners, *refs):
    keep, send = refs[-2:]
    low, high = refs[:owners], refs[owners : 2 * owners]
    swapped = (lax.axis_index("ctx") // owners ^ lax.axis_index("head")) & 1
    for flag, first, second in ((0, low, high), (1, high, low)):

        @pl.when(swapped == flag)
        def _(first=first, second=second):
            merge_kernel(blocks, width, *first, keep)
            merge_kernel(blocks, width, *second, send)


def merge_pair(low, high, blocks, width):
    return pl.pallas_call(
        functools.partial(pair_kernel, blocks, width, len(low)),
        out_shape=[jax.ShapeDtypeStruct(low[0].shape, low[0].dtype)] * 2,
        in_specs=[VMEM] * (2 * len(low)),
        out_specs=[VMEM] * 2,
        compiler_params=pltpu.CompilerParams(vmem_limit_bytes=4 << 20),
        cost_estimate=pl.CostEstimate(flops=low[0].size * 8, bytes_accessed=low[0].size * 12, transcendentals=0),
    )(*low, *high)


def finish_kernel(units, group, blocks, width, owners, *refs):
    out, held, sems = refs[-3:]
    size = section(blocks, width)
    picked = (lax.axis_index("ctx") // owners ^ lax.axis_index("head")) // 2
    for stage in range(1 + max(k for k, _, _ in units)):

        @pl.when(picked == stage)
        def _(stage=stage):
            at = 0
            copies = []
            for k, heads, many in units:
                if k == stage:
                    for n, g in enumerate(heads):
                        for i in range(many):
                            source = refs[at + i].at[pl.ds(n * size, size)]
                            copies.append(pltpu.make_async_copy(source, held.at[g, i], sems.at[g, i]))
                at += many
            for copy in copies:
                copy.start()
            for copy in copies:
                copy.wait()

    tokens = LANES // group
    for g in range(held.shape[0]):
        ins = [held.at[g, i] for i in range(held.shape[1])]
        shares, _ = merge_weights(ins, blocks * width)
        for b in range(blocks):
            value = merged(ins, shares, b * width, b, width)
            turned = value.T.astype(jnp.bfloat16).reshape(tokens, group, width)
            out[b * tokens : (b + 1) * tokens, g * group : (g + 1) * group, :] = turned


def finish(units, heads, group, blocks, width, owners):
    many = len(units[0][2])
    msgs = [msg for _, _, msgs in units for msg in msgs]
    shape = tuple((k, hs, len(ms)) for k, hs, ms in units)
    return pl.pallas_call(
        functools.partial(finish_kernel, shape, group, blocks, width, owners),
        out_shape=jax.ShapeDtypeStruct((blocks * LANES // group, heads * group, width), jnp.bfloat16),
        in_specs=[HBM] * len(msgs),
        out_specs=VMEM,
        scratch_shapes=[
            pltpu.VMEM((heads, many, section(blocks, width), width), jnp.bfloat16),
            pltpu.SemaphoreType.DMA((heads, many)),
        ],
        compiler_params=pltpu.CompilerParams(vmem_limit_bytes=8 << 20),
    )(*msgs)


def attend(table, scales, q, tiles, heads, group, owners, block):
    width = q.shape[2]
    rows = q.shape[0] * group
    blocks = rows // owners // LANES
    message = jax.ShapeDtypeStruct((len(heads) * section(blocks, width), width), jnp.bfloat16)
    likely = len(heads) * rows * 3 * PER_TILE * block
    return pl.pallas_call(
        functools.partial(attend_kernel, (heads, group, owners, block)),
        out_shape=[message] * owners,
        in_specs=[SMEM, SMEM, VMEM, VMEM],
        out_specs=[VMEM] * owners,
        scratch_shapes=[
            pltpu.VMEM((len(heads), width + PACK, rows), jnp.float32),
            pltpu.VMEM((len(heads), 1, rows), jnp.float32),
            pltpu.VMEM((8, LANES), jnp.float32),
        ],
        compiler_params=pltpu.CompilerParams(vmem_limit_bytes=16 << 20),
        cost_estimate=pl.CostEstimate(flops=4 * likely * width, bytes_accessed=4 << 20, transcendentals=likely),
    )(table, scales, q, tiles)


def plan_units(head_size, heads):
    pieces = [(p, tuple(range(heads))) for p in range(head_size // 2 - 1)]
    return pieces + [(head_size // 2 - 1, (g,)) for g in range(heads)]


def on_device(ctx_size, head_size, queries, keys, values, key_block_scale, value_block_scale, selection):
    heads, _, width = keys.shape
    local = key_block_scale.shape[1]
    block = keys.shape[1] // local
    group = queries.shape[1] // head_size // heads
    owners = ctx_size // head_size
    blocks = queries.shape[0] * group // owners // LANES

    chunks = list(part(keep_out(queries), head_size))
    for k in range(1, head_size):
        chunks[k] = lax.ppermute(chunks[k], "head", [(i, i ^ k) for i in range(head_size)])
    tiles, table, scales = collect(*map(keep_out, (selection, key_block_scale, value_block_scale, keys, values)))

    def index(c, h):
        return c * head_size + h

    units = []
    for p, hs in plan_units(head_size, heads):
        gathered = []
        for k in (2 * p, 2 * p + 1):
            msgs = attend(table, scales, chunks[k], tiles, hs, group, owners, block)
            got = [
                lax.ppermute(msgs[d], "ctx", [(c, c ^ d) for c in range(ctx_size)]) for d in range(1, owners)
            ]
            gathered.append([msgs[0]] + got)
        held, sent = merge_pair(*gathered, blocks, width)
        got = lax.ppermute(sent, "ctx", [(c, c ^ owners) for c in range(ctx_size)])
        for bit in range(1, head_size.bit_length() - 1):
            held = merge([held, got], blocks, width)
            routes = []
            step = 1 << bit
            for c in range(ctx_size):
                for h in range(head_size):
                    apart = (c // owners ^ h ^ 2 * p) & (2 * step - 2)
                    if apart == step:
                        routes.append((index(c, h), index(c ^ (step * owners), h)))
            got = lax.ppermute(held, ("ctx", "head"), routes)
        units.append((p, hs, [held, got]))
    return finish(units, heads, group, blocks, width, owners)


def solution(mesh):
    ctx_size, head_size = mesh.shape["ctx"], mesh.shape["head"]

    def body(*args):
        return on_device(ctx_size, head_size, *args)

    return jax.shard_map(
        body,
        mesh=mesh,
        in_specs=(
            P("head", None, None),
            P("head", "ctx", None),
            P("head", "ctx", None),
            P("head", "ctx"),
            P("head", "ctx"),
            P("head", None),
        ),
        out_specs=P("ctx", "head", None),
        check_vma=False,
    )
```

```python
import functools
import math

import jax
import jax.numpy as jnp
from jax import lax
from jax.experimental import pallas as pl
from jax.experimental.pallas import tpu as pltpu
from jax.sharding import PartitionSpec as P


MOST = 40
LANES = 128
PACK = 16
PARTS = 3
PER_TILE = 8
NEG = -1e30
SAFE = 2.0**64

SMEM = pl.BlockSpec(memory_space=pltpu.SMEM)
VMEM = pl.BlockSpec(memory_space=pltpu.VMEM)
HBM = pl.BlockSpec(memory_space=pltpu.HBM)


def keep_out(x):
    return pltpu.with_memory_space_constraint(x, pltpu.HBM)


def locate(sel_ref, wanted):
    length = sel_ref.shape[1]
    spans = [(jnp.int32(0), jnp.int32(length)) for _ in wanted]
    for _ in range(length.bit_length()):
        for n, (g, bound) in enumerate(wanted):
            low, high = spans[n]
            mid = (low + high) >> 1
            below = jnp.logical_and(low < high, sel_ref[g, jnp.minimum(mid, length - 1)] < bound)
            spans[n] = jnp.where(below, mid + 1, low), jnp.where(below, high, jnp.minimum(mid, high))
    return [low for low, _ in spans]


def collect_kernel(block, local, sel_ref, ks_ref, vs_ref, k_hbm, v_hbm, tiles, table, scales, vbuf, ksem, vsem):
    heads, _, width = k_hbm.shape
    most = (tiles.shape[0]) // heads
    keys = PER_TILE * block
    factor = math.log2(math.e) / math.sqrt(width)
    base = lax.axis_index("ctx") * local
    spans = []
    start = jnp.int32(0)
    bounds = locate(sel_ref, [(g, base + end) for g in range(heads) for end in (0, local)])
    for g in range(heads):
        first = bounds[2 * g]
        count = bounds[2 * g + 1] - first
        turns = jnp.minimum((count + PER_TILE - 1) // PER_TILE, most)
        table[g] = start
        spans.append((first, count, turns, start))
        start = start + turns
    table[heads] = start

    for g in range(heads):
        first, count, turns, start = spans[g]

        def fetch(t, _, g=g, first=first, count=count, start=start):
            i = start + t
            for b in range(PER_TILE):
                slot = t * PER_TILE + b
                at = sel_ref[g, first + jnp.minimum(slot, count - 1)] - base
                source = pl.ds(pl.multiple_of(at * block, block), block)
                target = pl.ds(b * block, block)
                pltpu.make_async_copy(v_hbm.at[g, source], vbuf.at[i, target], vsem.at[i]).start()
                pltpu.make_async_copy(k_hbm.at[g, source], tiles.at[i, target], ksem.at[i]).start()
                scales[i, b] = ks_ref[g, at] * factor
            return 0

        lax.fori_loop(0, turns, fetch, 0)

    for g in range(heads):
        first, count, turns, start = spans[g]

        def turn(t, _, g=g, first=first, count=count, start=start):
            i = start + t
            some = pl.ds(0, keys)
            pltpu.make_async_copy(v_hbm.at[g, some], vbuf.at[i], vsem.at[i]).wait()
            for b in range(0, PER_TILE, LANES // block):
                rows = []
                for c in range(b, b + LANES // block):
                    slot = t * PER_TILE + c
                    at = sel_ref[g, first + jnp.minimum(slot, count - 1)] - base
                    scale = jnp.where(slot < count, vs_ref[g, at], 0.0)
                    rows.append(vbuf[i, c * block : (c + 1) * block, :].astype(jnp.float32) * scale)
                key_at = lax.broadcasted_iota(jnp.int32, (PACK, LANES), 1) + (t * keys + b * block)
                live = jnp.where(key_at < count * block, 1.0, 0.0).astype(jnp.bfloat16)
                at = keys + b * block // LANES * (width + PACK)
                tiles[i, at : at + width, :] = jnp.concatenate(rows, axis=0).T.astype(jnp.bfloat16)
                tiles[i, at + width : at + width + PACK, :] = live
            pltpu.make_async_copy(k_hbm.at[g, some], tiles.at[i, some], ksem.at[i]).wait()
            return 0

        lax.fori_loop(0, turns, turn, 0)


def collect(selection, key_scale, value_scale, k, v):
    heads, _, width = k.shape
    local = key_scale.shape[1]
    block = k.shape[1] // local
    keys = PER_TILE * block
    most = -(-min(MOST, local) // PER_TILE) * heads
    height = keys + keys // LANES * (width + PACK)
    return pl.pallas_call(
        functools.partial(collect_kernel, block, local),
        out_shape=[
            jax.ShapeDtypeStruct((most, height, width), jnp.bfloat16),
            jax.ShapeDtypeStruct((heads + 1,), jnp.int32),
            jax.ShapeDtypeStruct((most, PER_TILE), jnp.float32),
        ],
        in_specs=[SMEM, SMEM, SMEM, HBM, HBM],
        out_specs=[VMEM, SMEM, SMEM],
        scratch_shapes=[
            pltpu.VMEM((most, keys, width), jnp.bfloat16),
            pltpu.SemaphoreType.DMA((most,)),
            pltpu.SemaphoreType.DMA((most,)),
        ],
        compiler_params=pltpu.CompilerParams(vmem_limit_bytes=16 << 20),
        cost_estimate=pl.CostEstimate(flops=0, bytes_accessed=6 << 20, transcendentals=0),
    )(selection, key_scale, value_scale, k, v)


def attend_kernel(cfg, table, scales, q_ref, tiles, *rest):
    heads, group, owners, block = cfg
    msgs = rest[:owners]
    acc, m_scr, lse_scr = rest[owners:]
    keys = PER_TILE * block
    width = tiles.shape[-1]
    rows = acc.shape[2]
    low, high = table[heads[0]], table[heads[-1] + 1]

    def query(g):
        return q_ref[:, pl.ds(pl.multiple_of(g * group, group), group), :].reshape(rows, width)

    def score(k, q):
        return lax.dot_general(k, q, (((1,), (1,)), ((), ())), preferred_element_type=jnp.float32)

    def head_of(i):
        g = jnp.int32(heads[0])
        for h in heads[1:]:
            g = g + (i >= table[h]).astype(jnp.int32)
        return g

    def scaled(i, q):
        s = score(tiles[i, :keys, :], q)
        return [s[b * block : (b + 1) * block] * scales[i, b] for b in range(PER_TILE)]

    def values(i):
        step = width + PACK
        parts = [tiles[i, keys + c * step : keys + (c + 1) * step, :] for c in range(keys // LANES)]
        return jnp.concatenate(parts, axis=1)

    def quick(i, _):
        g = head_of(i)
        at = g - heads[0]
        m = m_scr[at]
        weights = [jnp.exp2(x - m).astype(jnp.bfloat16) for x in scaled(i, query(g))]
        acc[at] += jnp.dot(values(i), jnp.concatenate(weights, axis=0), preferred_element_type=jnp.float32)
        return 0

    def careful(i, _):
        g = head_of(i)
        at = g - heads[0]
        s = scaled(i, query(g))
        old = m_scr[at]
        new = jnp.maximum(old, jnp.max(functools.reduce(jnp.maximum, s), axis=0, keepdims=True))
        weights = jnp.concatenate([jnp.exp2(x - new).astype(jnp.bfloat16) for x in s], axis=0)
        acc[at] = acc[at] * jnp.exp2(old - new) + jnp.dot(
            values(i), weights, preferred_element_type=jnp.float32
        )
        m_scr[at] = new
        return 0

    acc[...] = jnp.zeros_like(acc)
    for n, g in enumerate(heads):
        first = table[g]
        q = q_ref[:, g * group : (g + 1) * group, :].reshape(rows, width)
        m_scr[n] = jnp.max(score(tiles[first, :block, :], q), axis=0, keepdims=True) * scales[first, 0]
    lax.fori_loop(low, high, quick, 0)

    @pl.when(jnp.logical_not(jnp.max(acc[:, width : width + 1, :]) < SAFE))
    def _():
        acc[...] = jnp.zeros_like(acc)
        m_scr[...] = jnp.full_like(m_scr, NEG)
        lax.fori_loop(low, high, careful, 0)

    blocks = rows // owners // LANES
    size = section(blocks, width)
    for d in range(owners):
        x = lax.rem(lax.axis_index("ctx"), owners) ^ d
        for n in range(len(heads)):
            for b in range(blocks):
                at = pl.ds(pl.multiple_of((x * blocks + b) * LANES, LANES), LANES)
                total = acc[n, width : width + 1, at]
                row = n * size + b * width
                msgs[d][row : row + width, :] = (acc[n, :width, at] * (1.0 / total)).astype(jnp.bfloat16)
                lse_scr[b : b + 1, :] = m_scr[n, :, at] + jnp.log2(total)
            put_level(msgs[d], lse_scr[...], n * size + blocks * width)


def section(blocks, width):
    return blocks * width + PARTS * PACK


def put_level(msg_ref, level, at):
    for i in range(PARTS):
        part = level.astype(jnp.bfloat16)
        msg_ref[at + i * PACK : at + i * PACK + level.shape[0], :] = part
        level = level - part.astype(jnp.float32)


def get_level(msg_ref, at):
    parts = [msg_ref[at + i * PACK : at + i * PACK + 8, :].astype(jnp.float32) for i in range(PARTS)]
    return functools.reduce(jnp.add, parts)


def merge_weights(refs, at):
    levels = [get_level(ref, at) for ref in refs]
    peak = functools.reduce(jnp.maximum, levels)
    shares = [jnp.exp2(level - peak) for level in levels]
    whole = functools.reduce(jnp.add, shares)
    return [share / whole for share in shares], peak + jnp.log2(whole)


def merged(refs, shares, row, b, width):
    values = [ref[row : row + width, :].astype(jnp.float32) * share[b : b + 1] for ref, share in zip(refs, shares)]
    return functools.reduce(jnp.add, values)


def merge_kernel(blocks, width, *refs):
    out = refs[-1]
    ins = refs[:-1]
    size = section(blocks, width)
    for n in range(out.shape[0] // size):
        shares, level = merge_weights(ins, n * size + blocks * width)
        for b in range(blocks):
            row = n * size + b * width
            out[row : row + width, :] = merged(ins, shares, row, b, width).astype(jnp.bfloat16)
        put_level(out, level, n * size + blocks * width)


def merge(msgs, blocks, width):
    return pl.pallas_call(
        functools.partial(merge_kernel, blocks, width),
        out_shape=jax.ShapeDtypeStruct(msgs[0].shape, msgs[0].dtype),
        in_specs=[VMEM] * len(msgs),
        out_specs=VMEM,
        compiler_params=pltpu.CompilerParams(vmem_limit_bytes=4 << 20),
        cost_estimate=pl.CostEstimate(flops=msgs[0].size * 4, bytes_accessed=msgs[0].size * 6, transcendentals=0),
    )(*msgs)


def part_kernel(group, q_hbm, *refs):
    chunks, sems = refs[:-1], refs[-1]
    copies = []
    for k, chunk in enumerate(chunks):
        at = pl.multiple_of((lax.axis_index("head") ^ k) * group, group)
        copies.append(pltpu.make_async_copy(q_hbm.at[:, pl.ds(at, group), :], chunk, sems.at[k]))
    for copy in copies:
        copy.start()
    for copy in copies:
        copy.wait()


def part(queries, many):
    tokens, heads, width = queries.shape
    return pl.pallas_call(
        functools.partial(part_kernel, heads // many),
        out_shape=[jax.ShapeDtypeStruct((tokens, heads // many, width), queries.dtype)] * many,
        in_specs=[HBM],
        out_specs=[VMEM] * many,
        scratch_shapes=[pltpu.SemaphoreType.DMA((many,))],
        compiler_params=pltpu.CompilerParams(vmem_limit_bytes=16 << 20),
    )(queries)


def pair_kernel(blocks, width, owners, *refs):
    keep, send = refs[-2:]
    low, high = refs[:owners], refs[owners : 2 * owners]
    swapped = (lax.axis_index("ctx") // owners ^ lax.axis_index("head")) & 1
    for flag, first, second in ((0, low, high), (1, high, low)):

        @pl.when(swapped == flag)
        def _(first=first, second=second):
            merge_kernel(blocks, width, *first, keep)
            merge_kernel(blocks, width, *second, send)


def merge_pair(low, high, blocks, width):
    return pl.pallas_call(
        functools.partial(pair_kernel, blocks, width, len(low)),
        out_shape=[jax.ShapeDtypeStruct(low[0].shape, low[0].dtype)] * 2,
        in_specs=[VMEM] * (2 * len(low)),
        out_specs=[VMEM] * 2,
        compiler_params=pltpu.CompilerParams(vmem_limit_bytes=4 << 20),
        cost_estimate=pl.CostEstimate(flops=low[0].size * 8, bytes_accessed=low[0].size * 12, transcendentals=0),
    )(*low, *high)


def finish_kernel(units, group, blocks, width, owners, *refs):
    out, held, sems = refs[-3:]
    size = section(blocks, width)
    picked = (lax.axis_index("ctx") // owners ^ lax.axis_index("head")) // 2
    for stage in range(1 + max(k for k, _, _ in units)):

        @pl.when(picked == stage)
        def _(stage=stage):
            at = 0
            copies = []
            for k, heads, many in units:
                if k == stage:
                    for n, g in enumerate(heads):
                        for i in range(many):
                            source = refs[at + i].at[pl.ds(n * size, size)]
                            copies.append(pltpu.make_async_copy(source, held.at[g, i], sems.at[g, i]))
                at += many
            for copy in copies:
                copy.start()
            for copy in copies:
                copy.wait()

    tokens = LANES // group
    for g in range(held.shape[0]):
        ins = [held.at[g, i] for i in range(held.shape[1])]
        shares, _ = merge_weights(ins, blocks * width)
        for b in range(blocks):
            value = merged(ins, shares, b * width, b, width)
            turned = value.T.astype(jnp.bfloat16).reshape(tokens, group, width)
            out[b * tokens : (b + 1) * tokens, g * group : (g + 1) * group, :] = turned


def finish(units, heads, group, blocks, width, owners):
    many = len(units[0][2])
    msgs = [msg for _, _, msgs in units for msg in msgs]
    shape = tuple((k, hs, len(ms)) for k, hs, ms in units)
    return pl.pallas_call(
        functools.partial(finish_kernel, shape, group, blocks, width, owners),
        out_shape=jax.ShapeDtypeStruct((blocks * LANES // group, heads * group, width), jnp.bfloat16),
        in_specs=[HBM] * len(msgs),
        out_specs=VMEM,
        scratch_shapes=[
            pltpu.VMEM((heads, many, section(blocks, width), width), jnp.bfloat16),
            pltpu.SemaphoreType.DMA((heads, many)),
        ],
        compiler_params=pltpu.CompilerParams(vmem_limit_bytes=8 << 20),
    )(*msgs)


def attend(table, scales, q, tiles, heads, group, owners, block):
    width = q.shape[2]
    rows = q.shape[0] * group
    blocks = rows // owners // LANES
    message = jax.ShapeDtypeStruct((len(heads) * section(blocks, width), width), jnp.bfloat16)
    likely = len(heads) * rows * 3 * PER_TILE * block
    return pl.pallas_call(
        functools.partial(attend_kernel, (heads, group, owners, block)),
        out_shape=[message] * owners,
        in_specs=[SMEM, SMEM, VMEM, VMEM],
        out_specs=[VMEM] * owners,
        scratch_shapes=[
            pltpu.VMEM((len(heads), width + PACK, rows), jnp.float32),
            pltpu.VMEM((len(heads), 1, rows), jnp.float32),
            pltpu.VMEM((8, LANES), jnp.float32),
        ],
        compiler_params=pltpu.CompilerParams(vmem_limit_bytes=16 << 20),
        cost_estimate=pl.CostEstimate(flops=4 * likely * width, bytes_accessed=4 << 20, transcendentals=likely),
    )(table, scales, q, tiles)


def plan_units(head_size, heads):
    pieces = [(p, tuple(range(heads))) for p in range(head_size // 2 - 1)]
    return pieces + [(head_size // 2 - 1, (g,)) for g in range(heads)]


def on_device(ctx_size, head_size, queries, keys, values, key_block_scale, value_block_scale, selection):
    heads, _, width = keys.shape
    local = key_block_scale.shape[1]
    block = keys.shape[1] // local
    group = queries.shape[1] // head_size // heads
    owners = ctx_size // head_size
    blocks = queries.shape[0] * group // owners // LANES

    chunks = list(part(keep_out(queries), head_size))
    for k in range(1, head_size):
        chunks[k] = lax.ppermute(chunks[k], "head", [(i, i ^ k) for i in range(head_size)])
    tiles, table, scales = collect(*map(keep_out, (selection, key_block_scale, value_block_scale, keys, values)))

    def index(c, h):
        return c * head_size + h

    units = []
    for p, hs in plan_units(head_size, heads):
        gathered = []
        for k in (2 * p, 2 * p + 1):
            msgs = attend(table, scales, chunks[k], tiles, hs, group, owners, block)
            got = [
                lax.ppermute(msgs[d], "ctx", [(c, c ^ d) for c in range(ctx_size)]) for d in range(1, owners)
            ]
            gathered.append([msgs[0]] + got)
        held, sent = merge_pair(*gathered, blocks, width)
        got = lax.ppermute(sent, "ctx", [(c, c ^ owners) for c in range(ctx_size)])
        for bit in range(1, head_size.bit_length() - 1):
            held = merge([held, got], blocks, width)
            routes = []
            step = 1 << bit
            for c in range(ctx_size):
                for h in range(head_size):
                    apart = (c // owners ^ h ^ 2 * p) & (2 * step - 2)
                    if apart == step:
                        routes.append((index(c, h), index(c ^ (step * owners), h)))
            got = lax.ppermute(held, ("ctx", "head"), routes)
        units.append((p, hs, [held, got]))
    return finish(units, heads, group, blocks, width, owners)


def solution(mesh):
    ctx_size, head_size = mesh.shape["ctx"], mesh.shape["head"]

    def body(*args):
        return on_device(ctx_size, head_size, *args)

    return jax.shard_map(
        body,
        mesh=mesh,
        in_specs=(
            P("head", None, None),
            P("head", "ctx", None),
            P("head", "ctx", None),
            P("head", "ctx"),
            P("head", "ctx"),
            P("head", None),
        ),
        out_specs=P("ctx", "head", None),
        check_vma=False,
    )
```
